1024 devices in a mesh: row: 16 (over x_hi, y, core), col: 64 (over z, x_lo).
Axes of the slice: x: 4 (x_hi: 2, x_lo: 2; x = x_hi * 2 + x_lo), y: 4, z: 32, core: 2. Of those that a mesh axis runs over, the one named last changes fastest.
Arguments:
- start_block: bfloat16 [131072, 128], P(('row', 'col')), may hold values from -6 to 6
- matrix_tiles: bfloat16 [16, 16, 64, 2, 128, 128], P('row', None, 'col')
- tile_columns: int32 [16, 16, 64, 2], P('row', None, 'col'), may hold values from 0 to 63
- history: bfloat16 [131072, 512], P(('row', 'col'))
Outputs:
- new_block: float32 [131072, 128], P(('row', 'col'))
- coeffs: float32 [512, 128], replicated
The draws below stay inside these ranges and needn't reach their ends.
All inputs are finite; a program needn't handle non-finite values.
Results may differ from the reference program's by a relative error of at most 0.0029.
Values may be sent and summed in bfloat16 or wider, within the bound.
A program may use at most 32 MiB of HBM per device.

```python
import jax
import jax.numpy as jnp
from jax import lax

TILE = 128
K = 128
SLOTS = 2
M = 512
NS = 131072
N_ROW = 16
N_COL = 64


def draw_matrix_tiles(key, part):
    full_shape = (N_ROW, N_ROW, N_COL, SLOTS, TILE, TILE)
    position = (jnp.arange(N_ROW)[:, None] * N_COL + jnp.arange(N_COL)[None, :]).astype(jnp.float32)
    fraction = position / (N_ROW * N_COL - 1)
    values = jnp.clip(jax.random.normal(key, full_shape, jnp.float32), -6.0, 6.0)
    spread = jnp.exp(jnp.log(0.3) + jnp.log(10.0) * fraction)
    factor = spread[None, :, :, None, None, None] / jnp.sqrt(jnp.float32(N_ROW * SLOTS * TILE))
    return (values * factor).astype(jnp.bfloat16)


def draw_history(key, part):
    noise_key = jax.random.fold_in(key, 11)
    shared_key = jax.random.fold_in(key, 12)
    loading_key = jax.random.fold_in(key, 13)
    noise = jnp.clip(jax.random.normal(noise_key, (NS, M), jnp.float32), -6.0, 6.0)
    shared = jnp.clip(jax.random.normal(shared_key, (NS,), jnp.float32), -6.0, 6.0)
    loading = jnp.clip(jax.random.normal(loading_key, (M,), jnp.float32), -6.0, 6.0)
    share = 0.15
    strength = jnp.sqrt(jnp.sqrt(jnp.float32(share * NS)) / jnp.float32(M))
    mixed = noise + strength * shared[:, None] * loading[None, :]
    return (mixed / jnp.sqrt(jnp.float32(NS))).astype(jnp.bfloat16)


def place_ends(array, rng, least, largest):
    longest = array.shape.index(max(array.shape))
    spots = []
    for shift in (0, 1):
        where = [jax.random.randint(jax.random.fold_in(rng, axis), (), 0, length) for axis, length in enumerate(array.shape)]
        where[longest] = (where[longest] + shift) % array.shape[longest]
        spots.append(tuple(where))
    return array.at[spots[0]].set(least).at[spots[1]].set(largest)


def levels(rng, dims, pieces, smallest, top_value):
    level = 1.0
    for dim, blocks in pieces:
        heights = jax.random.uniform(jax.random.fold_in(jax.random.fold_in(rng, 6), dim), (blocks,), jnp.float32, smallest / len(pieces), top_value / len(pieces))
        level = level * jnp.repeat(jnp.exp(heights), dims[dim] // blocks).reshape((-1,) + (1,) * (len(dims) - 1 - dim))
    return level


def scatter_about(stream_key, shape, deviation, most, pieces=(), kind=jnp.bfloat16):
    array = jax.random.normal(stream_key, shape, jnp.float32) * deviation
    if len(pieces) > 0:
        array = levels(stream_key, shape, pieces, -0.22, 0.18) * array
    return jnp.clip(array, min=-most, max=most).astype(kind)


def setup_inputs(seed: int = 0) -> dict:
    seeds = jax.random.split(jax.random.key(seed), 5)
    start_block = scatter_about(seeds[0], (NS, K), 1.0, 6.0, ((0, 1024),))
    matrix_tiles = draw_matrix_tiles(jax.random.fold_in(seeds[4], 71), 0)
    tile_columns = place_ends(jax.random.randint(seeds[2], (N_ROW, N_ROW, N_COL, SLOTS), 0, N_COL), jax.random.fold_in(seeds[2], 1), 0, N_COL - 1).astype(jnp.int32)
    history = draw_history(jax.random.fold_in(seeds[4], 71), 0)
    return dict(start_block=start_block, matrix_tiles=matrix_tiles, tile_columns=tile_columns, history=history)


def apply_matrix(vectors, matrix_tiles, tile_columns):

    def add_block(running, block_index):
        vector_block = lax.dynamic_slice_in_dim(vectors, block_index * (N_COL * TILE), N_COL * TILE, 0).reshape(N_COL, TILE, K)
        column_ids = lax.dynamic_index_in_dim(tile_columns, block_index, 0, keepdims=False)
        picked = vector_block[column_ids]
        tiles_here = lax.dynamic_index_in_dim(matrix_tiles, block_index, 0, keepdims=False)
        product = jnp.einsum('rcsij,rcsjk->rcik', tiles_here.astype(jnp.float32), picked.astype(jnp.float32))
        return (running + product, None)
    starting = jnp.zeros((N_ROW, N_COL, TILE, K), jnp.float32)
    summed, unused = lax.scan(add_block, starting, jnp.arange(N_ROW, dtype=jnp.int32))
    return summed.reshape(N_ROW * N_COL * TILE, K)

def reference(start_block, matrix_tiles, tile_columns, history):
    first_power = apply_matrix(start_block, matrix_tiles, tile_columns).astype(jnp.bfloat16)
    second_power = apply_matrix(first_power, matrix_tiles, tile_columns)
    filtered = 2.0 * second_power - start_block.astype(jnp.float32)
    history_wide = history.astype(jnp.float32)
    coeffs = jnp.dot(history_wide.T, filtered, precision=lax.Precision.HIGHEST)
    cleaned = filtered - jnp.dot(history_wide, coeffs, precision=lax.Precision.HIGHEST)
    lengths = jnp.sqrt(lax.optimization_barrier(jnp.mean(cleaned * cleaned, axis=0)) + 1e-05)
    return (cleaned / lengths[None, :], coeffs)
```

```python
import functools

import jax
import jax.numpy as jnp
from jax import lax
from jax.experimental import pallas as pl
from jax.experimental.pallas import tpu as pltpu
from jax.sharding import Mesh
from jax.sharding import PartitionSpec as P

COL = ("col_0", "col_1")
ROW = ("row_0", "row_1", "row_2")
ROW_COL = ROW + COL
MESH = pl.DeviceIdType.MESH
XH, Y, CORE, Z, XL = 2, 4, 2, 32, 2
ZA = 8
ZB = Z // ZA
PLANE = XH * XL * Y * CORE
TILE = 128


def split3(x):
    hi = x.astype(jnp.bfloat16)
    rest = x - hi.astype(jnp.float32)
    mid = rest.astype(jnp.bfloat16)
    low = (rest - mid.astype(jnp.float32)).astype(jnp.bfloat16)
    return hi, mid, low


def wait_bytes(ref, sem):
    pltpu.make_async_copy(ref, ref, sem).wait()


def kernel(
    states,
    cols,
    start,
    tiles,
    hist,
    out,
    coef_out,
    seg1,
    seg2,
    part,
    core_in,
    summed,
    y_in,
    pair,
    x_in,
    filt,
    proj,
    proj_in,
    za_in,
    zb_in,
    coef,
    sq_plane,
    sq_z,
    ring_send,
    ring_recv,
    row_send,
    row_recv,
    group_send,
    group_recv,
    local_sem,
):
    xh, y, core = (lax.axis_index(a) for a in ROW)
    z, xl = (lax.axis_index(a) for a in COL)
    right = (xh, y, core, lax.rem(z + 1, Z), xl)
    left = (xh, y, core, lax.rem(z + Z - 1, Z), xl)
    across = (xh, y, core, z, 1 - xl)
    place = ((xh * XL + xl) * Y + y) * CORE + core

    def plane_device(q):
        return (
            q // (XL * Y * CORE),
            lax.rem(q // CORE, Y),
            lax.rem(q, CORE),
            z,
            lax.rem(q // (Y * CORE), XL),
        )

    barrier = pltpu.get_barrier_semaphore()

    def greet(i, carry):
        device = plane_device(lax.rem(place + i, PLANE))
        pl.semaphore_signal(barrier, inc=1, device_id=device, device_id_type=MESH)
        return carry

    for device in (left, right):
        pl.semaphore_signal(barrier, inc=1, device_id=device, device_id_type=MESH)
    lax.fori_loop(1, PLANE, greet, 0)
    pl.semaphore_wait(barrier, PLANE + 1)

    def slot_of(zz):
        return lax.rem(zz + Z, Z) * XL + xl

    def gather(seg, which):
        def send(slot, device, lane):
            pltpu.make_async_remote_copy(
                src_ref=seg.at[slot],
                dst_ref=seg.at[slot],
                send_sem=ring_send.at[which, lane],
                recv_sem=ring_recv.at[which, slot],
                device_id=device,
                device_id_type=MESH,
            ).start()

        def arrived(slot):
            wait_bytes(seg.at[slot], ring_recv.at[which, slot])

        def step(k, carry):
            ahead, behind = slot_of(z - k), slot_of(z + k)
            send(ahead, right, 0)
            send(behind, left, 1)
            send(ahead, across, 2)

            @pl.when(k > 0)
            def _():
                send(behind, across, 2)

            arrived(slot_of(z - k - 1))
            arrived(slot_of(z + k + 1))
            return carry

        half = Z // 2
        lax.fori_loop(0, half - 1, step, 0)
        send(slot_of(z - half + 1), right, 0)
        send(slot_of(z - half + 1), across, 2)
        send(slot_of(z + half - 1), across, 2)
        arrived(slot_of(z - half))
        send(slot_of(z - half), across, 2)

        def other(zz, carry):
            arrived(zz * XL + 1 - xl)
            return carry

        lax.fori_loop(0, Z, other, 0)
        wait_bytes(seg.at[pl.ds(0, half)], ring_send.at[which, 0])
        wait_bytes(seg.at[pl.ds(0, half - 1)], ring_send.at[which, 1])
        wait_bytes(seg.at[pl.ds(0, Z)], ring_send.at[which, 2])

    def multiply(seg, which):
        def one(owner_core, yy, xx):
            p = (xx * Y + yy) * CORE + owner_core
            total = jnp.dot(
                tiles[p, 0], seg[cols[p, 0]], preferred_element_type=jnp.float32
            )
            total += jnp.dot(
                tiles[p, 1], seg[cols[p, 1]], preferred_element_type=jnp.float32
            )
            part[owner_core, yy, xx] = total

        def half_of(owner_core):
            def body(yy, carry):
                for xx in range(XH):
                    one(owner_core, yy, xx)
                return carry

            lax.fori_loop(0, Y, body, 0)

        half_of(1 - core)
        swap = pltpu.make_async_remote_copy(
            src_ref=part.at[1 - core],
            dst_ref=core_in.at[which],
            send_sem=row_send.at[which, 0],
            recv_sem=row_recv.at[which, 0],
            device_id=(xh, y, 1 - core, z, xl),
            device_id_type=MESH,
        )
        swap.start()
        half_of(core)
        swap.wait()

        def add_up(yy, carry):
            summed[yy] = part[core, yy] + core_in[which, yy]
            return carry

        lax.fori_loop(0, Y, add_up, 0)
        hops = []
        for i in (2, 1, 3):
            hops.append(
                pltpu.make_async_remote_copy(
                    src_ref=summed.at[lax.rem(y + i, Y)],
                    dst_ref=y_in.at[which, i - 1],
                    send_sem=row_send.at[which, i],
                    recv_sem=row_recv.at[which, i],
                    device_id=(xh, lax.rem(y + i, Y), core, z, xl),
                    device_id_type=MESH,
                )
            )
        for hop in hops:
            hop.start()
        for hop in hops:
            hop.wait()
        pair[...] = summed[y] + y_in[which, 0] + y_in[which, 1] + y_in[which, 2]
        last = pltpu.make_async_remote_copy(
            src_ref=pair.at[1 - xh],
            dst_ref=x_in.at[which],
            send_sem=row_send.at[which, Y],
            recv_sem=row_recv.at[which, Y],
            device_id=(1 - xh, y, core, z, xl),
            device_id_type=MESH,
        )
        last.start()
        last.wait()
        return pair[xh] + x_in[which]

    mine = slot_of(z)
    first = pltpu.make_async_copy(start, seg1.at[mine], local_sem)
    first.start()
    first.wait()
    gather(seg1, 0)
    seg2[mine] = multiply(seg1, 0).astype(jnp.bfloat16)
    gather(seg2, 1)
    filtered = 2.0 * multiply(seg2, 1) - start[...].astype(jnp.float32)
    filt[...] = filtered

    def to_group(source, target, group, count, me, device_of, whole):
        def send(i, carry):
            peer = lax.rem(me + i, count)
            pltpu.make_async_remote_copy(
                src_ref=source.at[peer if whole else me],
                dst_ref=target.at[me],
                send_sem=group_send.at[group],
                recv_sem=group_recv.at[group],
                device_id=device_of(peer),
                device_id_type=MESH,
            ).start()
            return carry

        lax.fori_loop(1, count, send, 0)
        wait_bytes(target.at[pl.ds(0, count - 1)], group_recv.at[group])
        wait_bytes(target.at[pl.ds(0, count - 1)], group_send.at[group])

    def sum_of(ref, count):
        total = ref[0]
        for i in range(1, count):
            total = total + ref[i]
        return total

    total = None
    for term in split3(filtered):
        product = lax.dot_general(
            hist[...], term, (((0,), (0,)), ((), ())), preferred_element_type=jnp.float32
        )
        total = product if total is None else total + product
    proj[...] = total.reshape(proj.shape)
    proj_in[place] = proj[place]
    to_group(proj, proj_in, 0, PLANE, place, plane_device, True)

    z_hi, z_lo = z // ZA, lax.rem(z, ZA)
    za_in[z_lo] = sum_of(proj_in, PLANE)
    to_group(za_in, za_in, 1, ZA, z_lo, lambda i: (xh, y, core, z_hi * ZA + i, xl), False)
    zb_in[z_hi] = sum_of(za_in, ZA)
    to_group(zb_in, zb_in, 2, ZB, z_hi, lambda i: (xh, y, core, i * ZA + z_lo, xl), False)
    coef[place] = sum_of(zb_in, ZB)
    to_group(coef, coef, 3, PLANE, place, plane_device, False)
    coeffs = coef[...].reshape(coef_out.shape)
    coef_out[...] = coeffs

    cleaned = filt[...]
    for term in split3(coeffs):
        cleaned = cleaned - jnp.dot(hist[...], term, preferred_element_type=jnp.float32)
    filt[...] = cleaned
    sq_plane[place] = jnp.sum(cleaned * cleaned, axis=0, keepdims=True)
    to_group(sq_plane, sq_plane, 4, PLANE, place, plane_device, False)
    sq_z[z] = sum_of(sq_plane, PLANE)
    to_group(sq_z, sq_z, 5, Z, z, lambda i: (xh, y, core, i, xl), False)
    lengths = jnp.sqrt(sum_of(sq_z, Z) / states + 1e-05)
    out[...] = filt[...] / lengths


def per_device(start_block, matrix_tiles, tile_columns, history):
    rows, width = start_block.shape
    vectors = history.shape[1]
    chunk = vectors // PLANE
    f32, bf16 = jnp.float32, jnp.bfloat16
    vmem = pl.BlockSpec(memory_space=pltpu.VMEM)
    return pl.pallas_call(
        functools.partial(kernel, float(rows * XH * Y * CORE * Z * XL)),
        out_shape=(
            jax.ShapeDtypeStruct((rows, width), f32),
            jax.ShapeDtypeStruct((vectors, width), f32),
        ),
        in_specs=[pl.BlockSpec(memory_space=pltpu.SMEM), vmem, vmem, vmem],
        out_specs=(vmem, vmem),
        scratch_shapes=[
            pltpu.VMEM((Z * XL, rows, width), bf16),
            pltpu.VMEM((Z * XL, rows, width), bf16),
            pltpu.VMEM((CORE, Y, XH, rows, width), f32),
            pltpu.VMEM((2, Y, XH, rows, width), f32),
            pltpu.VMEM((Y, XH, rows, width), f32),
            pltpu.VMEM((2, Y - 1, XH, rows, width), f32),
            pltpu.VMEM((XH, rows, width), f32),
            pltpu.VMEM((2, rows, width), f32),
            pltpu.VMEM((rows, width), f32),
            pltpu.VMEM((PLANE, chunk, width), f32),
            pltpu.VMEM((PLANE, chunk, width), f32),
            pltpu.VMEM((ZA, chunk, width), f32),
            pltpu.VMEM((ZB, chunk, width), f32),
            pltpu.VMEM((PLANE, chunk, width), f32),
            pltpu.VMEM((PLANE, 1, width), f32),
            pltpu.VMEM((Z, 1, width), f32),
            pltpu.SemaphoreType.DMA((2, 3)),
            pltpu.SemaphoreType.DMA((2, Z * XL)),
            pltpu.SemaphoreType.DMA((2, Y + 1)),
            pltpu.SemaphoreType.DMA((2, Y + 1)),
            pltpu.SemaphoreType.DMA((6,)),
            pltpu.SemaphoreType.DMA((6,)),
            pltpu.SemaphoreType.DMA,
        ],
        compiler_params=pltpu.CompilerParams(
            collective_id=0, has_side_effects=True, vmem_limit_bytes=40 * 1024 * 1024
        ),
    )(
        tile_columns.reshape(XH * Y * CORE, 2),
        start_block,
        matrix_tiles.reshape(XH * Y * CORE, 2, TILE, TILE),
        history,
    )


def solution(mesh):
    split = Mesh(mesh.devices.reshape(XH, Y, CORE, Z, XL), ROW_COL)
    return jax.shard_map(
        per_device,
        mesh=split,
        in_specs=(
            P(ROW_COL, None),
            P(ROW, None, COL, None, None, None),
            P(ROW, None, COL, None),
            P(ROW_COL, None),
        ),
        out_specs=(P(ROW_COL, None), P()),
        check_vma=False,
    )
```

```python
import functools

import jax
import jax.numpy as jnp
from jax import lax
from jax.experimental import pallas as pl
from jax.experimental.pallas import tpu as pltpu
from jax.sharding import Mesh
from jax.sharding import PartitionSpec as P

COL = ("col_0", "col_1")
ROW = ("row_0", "row_1", "row_2")
ROW_COL = ROW + COL
MESH = pl.DeviceIdType.MESH
XH, Y, CORE, Z, XL = 2, 4, 2, 32, 2
ZA = 8
ZB = Z // ZA
PLANE = XH * XL * Y * CORE
TILE = 128
STRIDE = 4


def split3(x):
    hi = x.astype(jnp.bfloat16)
    rest = x - hi.astype(jnp.float32)
    mid = rest.astype(jnp.bfloat16)
    low = (rest - mid.astype(jnp.float32)).astype(jnp.bfloat16)
    return hi, mid, low


def wait_bytes(ref, sem):
    pltpu.make_async_copy(ref, ref, sem).wait()


def kernel(
    states,
    cols,
    start_hbm,
    tiles_hbm,
    hist_hbm,
    out,
    coef_out,
    start,
    tiles,
    hist,
    seg1,
    seg2,
    part,
    core_in,
    summed,
    y_in,
    pair,
    x_in,
    filt,
    proj,
    proj_in,
    za_in,
    zb_in,
    coef,
    sq_plane,
    sq_z,
    ring_send,
    ring_recv,
    row_send,
    row_recv,
    group_send,
    group_recv,
    local_sem,
):
    xh, y, core = (lax.axis_index(a) for a in ROW)
    z, xl = (lax.axis_index(a) for a in COL)

    def along(step):
        return (xh, y, core, lax.rem(z + step + Z, Z), xl)

    across = (xh, y, core, z, 1 - xl)
    place = ((xh * XL + xl) * Y + y) * CORE + core

    def plane_device(q):
        return (
            q // (XL * Y * CORE),
            lax.rem(q // CORE, Y),
            lax.rem(q, CORE),
            z,
            lax.rem(q // (Y * CORE), XL),
        )

    def slot_of(zz):
        return lax.rem(zz + 2 * Z, Z) * XL + xl

    mine = slot_of(z)
    first = pltpu.make_async_copy(start_hbm, seg1.at[mine], local_sem.at[0])
    first.start()
    loads = [
        pltpu.make_async_copy(source, target, local_sem.at[i])
        for i, source, target in (
            (1, tiles_hbm, tiles),
            (2, hist_hbm, hist),
            (3, start_hbm, start),
        )
    ]
    for load in loads:
        load.start()
    barrier = pltpu.get_barrier_semaphore()

    def greet(i, carry):
        device = plane_device(lax.rem(place + i, PLANE))
        pl.semaphore_signal(barrier, inc=1, device_id=device, device_id_type=MESH)
        return carry

    for reach in (STRIDE, 2, 1):
        for device in (along(reach), along(-reach)):
            pl.semaphore_signal(
                barrier, inc=1, device_id=device, device_id_type=MESH
            )
    lax.fori_loop(1, PLANE, greet, 0)
    pl.semaphore_wait(barrier, PLANE + 5)

    def gather(seg, which):
        def send(offset, device, lane):
            slot = slot_of(z + offset)
            pltpu.make_async_remote_copy(
                src_ref=seg.at[slot],
                dst_ref=seg.at[slot],
                send_sem=ring_send.at[which, lane],
                recv_sem=ring_recv.at[which, slot],
                device_id=device,
                device_id_type=MESH,
            ).start()

        def arrived(offset):
            slot = slot_of(z + offset)
            wait_bytes(seg.at[slot], ring_recv.at[which, slot])

        def cross(*offsets):
            for offset in offsets:
                arrived(offset)
                send(offset, across, 4)

        def spread(k):
            for near in (1, -1):
                send(-STRIDE * k, along(near), 2)
                send(STRIDE * k, along(near), 3)
            send(-STRIDE * k, along(2), 2)
            send(STRIDE * k, along(-2), 3)

        def spread_in(k):
            cross(-1 - STRIDE * k, 1 + STRIDE * k, -2 - STRIDE * k, 2 + STRIDE * k)

            @pl.when(k > 0)
            def _():
                cross(-1 + STRIDE * k, 1 - STRIDE * k)

        def step(k, carry):
            arrived(-STRIDE * k)
            send(-STRIDE * k, along(STRIDE), 0)
            arrived(STRIDE * k)
            send(STRIDE * k, along(-STRIDE), 1)
            spread(k)
            send(-STRIDE * k, across, 4)
            send(STRIDE * k, across, 4)
            spread_in(k - 1)
            return carry

        last = Z // 2 // STRIDE - 1
        far = Z // 2
        send(0, along(STRIDE), 0)
        send(0, along(-STRIDE), 1)
        send(0, along(1), 2)
        send(0, along(-1), 3)
        send(0, along(2), 2)
        send(0, along(-2), 3)
        send(0, across, 4)
        lax.fori_loop(1, last, step, 0)
        arrived(-STRIDE * last)
        send(-STRIDE * last, along(STRIDE), 0)
        arrived(STRIDE * last)
        spread(last)
        send(-STRIDE * last, across, 4)
        send(STRIDE * last, across, 4)
        spread_in(jnp.int32(last - 1))
        arrived(-far)
        send(-far, along(1), 2)
        send(-far, along(-1), 3)
        send(-far, across, 4)
        spread_in(jnp.int32(last))
        cross(far - 1, 1 - far)

        def other(zz, carry):
            slot = zz * XL + 1 - xl
            wait_bytes(seg.at[slot], ring_recv.at[which, slot])
            return carry

        lax.fori_loop(0, Z, other, 0)
        wait_bytes(seg.at[pl.ds(0, last + 1)], ring_send.at[which, 0])
        wait_bytes(seg.at[pl.ds(0, last)], ring_send.at[which, 1])
        wait_bytes(seg.at[pl.ds(0, 3 * last + 3)], ring_send.at[which, 2])
        wait_bytes(seg.at[pl.ds(0, 3 * last + 3)], ring_send.at[which, 3])
        wait_bytes(seg.at[pl.ds(0, Z)], ring_send.at[which, 4])

    def multiply(seg, which):
        def one(owner_core, yy, xx):
            p = (xx * Y + yy) * CORE + owner_core
            total = jnp.dot(
                tiles[p, 0], seg[cols[0, p]], preferred_element_type=jnp.float32
            )
            total += jnp.dot(
                tiles[p, 1], seg[cols[1, p]], preferred_element_type=jnp.float32
            )
            part[owner_core, yy, xx] = total

        def half_of(owner_core):
            def body(yy, carry):
                for xx in range(XH):
                    one(owner_core, yy, xx)
                return carry

            lax.fori_loop(0, Y, body, 0)

        half_of(1 - core)
        swap = pltpu.make_async_remote_copy(
            src_ref=part.at[1 - core],
            dst_ref=core_in.at[which],
            send_sem=row_send.at[which, 0],
            recv_sem=row_recv.at[which, 0],
            device_id=(xh, y, 1 - core, z, xl),
            device_id_type=MESH,
        )
        swap.start()
        half_of(core)
        swap.wait()

        def add_up(yy, carry):
            summed[yy] = part[core, yy] + core_in[which, yy]
            return carry

        lax.fori_loop(0, Y, add_up, 0)
        hops = []
        for i in (2, 1, 3):
            hops.append(
                pltpu.make_async_remote_copy(
                    src_ref=summed.at[lax.rem(y + i, Y)],
                    dst_ref=y_in.at[which, i - 1],
                    send_sem=row_send.at[which, i],
                    recv_sem=row_recv.at[which, i],
                    device_id=(xh, lax.rem(y + i, Y), core, z, xl),
                    device_id_type=MESH,
                )
            )
        for hop in hops:
            hop.start()
        for hop in hops:
            hop.wait()
        pair[...] = summed[y] + y_in[which, 0] + y_in[which, 1] + y_in[which, 2]
        last = pltpu.make_async_remote_copy(
            src_ref=pair.at[1 - xh],
            dst_ref=x_in.at[which],
            send_sem=row_send.at[which, Y],
            recv_sem=row_recv.at[which, Y],
            device_id=(1 - xh, y, core, z, xl),
            device_id_type=MESH,
        )
        last.start()
        last.wait()
        return pair[xh] + x_in[which]

    first.wait()
    gather(seg1, 0)
    for load in loads:
        load.wait()
    seg2[mine] = multiply(seg1, 0).astype(jnp.bfloat16)
    gather(seg2, 1)
    filtered = 2.0 * multiply(seg2, 1) - start[...].astype(jnp.float32)
    filt[...] = filtered

    def to_group(source, target, group, count, me, device_of, whole):
        def send(i, carry):
            peer = lax.rem(me + i, count)
            pltpu.make_async_remote_copy(
                src_ref=source.at[peer if whole else me],
                dst_ref=target.at[me],
                send_sem=group_send.at[group],
                recv_sem=group_recv.at[group],
                device_id=device_of(peer),
                device_id_type=MESH,
            ).start()
            return carry

        lax.fori_loop(1, count, send, 0)
        wait_bytes(target.at[pl.ds(0, count - 1)], group_recv.at[group])
        wait_bytes(target.at[pl.ds(0, count - 1)], group_send.at[group])

    def sum_of(ref, count):
        total = ref[0]
        for i in range(1, count):
            total = total + ref[i]
        return total

    total = None
    for term in split3(filtered):
        product = lax.dot_general(
            hist[...], term, (((0,), (0,)), ((), ())), preferred_element_type=jnp.float32
        )
        total = product if total is None else total + product
    proj[...] = total.reshape(proj.shape)
    proj_in[place] = proj[place]
    to_group(proj, proj_in, 0, PLANE, place, plane_device, True)

    z_hi, z_lo = z // ZA, lax.rem(z, ZA)
    za_in[z_lo] = sum_of(proj_in, PLANE)
    to_group(za_in, za_in, 1, ZA, z_lo, lambda i: (xh, y, core, z_hi * ZA + i, xl), False)
    zb_in[z_hi] = sum_of(za_in, ZA)
    to_group(zb_in, zb_in, 2, ZB, z_hi, lambda i: (xh, y, core, i * ZA + z_lo, xl), False)
    coef[place] = sum_of(zb_in, ZB)
    to_group(coef, coef, 3, PLANE, place, plane_device, False)
    coeffs = coef[...].reshape(coef_out.shape)
    coef_out[...] = coeffs

    cleaned = filt[...]
    for term in split3(coeffs):
        cleaned = cleaned - jnp.dot(hist[...], term, preferred_element_type=jnp.float32)
    filt[...] = cleaned
    sq_plane[place] = jnp.sum(cleaned * cleaned, axis=0, keepdims=True)
    to_group(sq_plane, sq_plane, 4, PLANE, place, plane_device, False)
    sq_z[z] = sum_of(sq_plane, PLANE)
    to_group(sq_z, sq_z, 5, Z, z, lambda i: (xh, y, core, i, xl), False)
    lengths = jnp.sqrt(sum_of(sq_z, Z) / states + 1e-05)
    out[...] = filt[...] / lengths


def per_device(start_block, matrix_tiles, tile_columns, history):
    rows, width = start_block.shape
    vectors = history.shape[1]
    chunk = vectors // PLANE
    f32, bf16 = jnp.float32, jnp.bfloat16
    vmem = pl.BlockSpec(memory_space=pltpu.VMEM)
    any_space = pl.BlockSpec(memory_space=pl.ANY)
    return pl.pallas_call(
        functools.partial(kernel, float(rows * XH * Y * CORE * Z * XL)),
        out_shape=(
            jax.ShapeDtypeStruct((rows, width), f32),
            jax.ShapeDtypeStruct((vectors, width), f32),
        ),
        in_specs=[pl.BlockSpec(memory_space=pltpu.SMEM), any_space, any_space, any_space],
        out_specs=(vmem, vmem),
        scratch_shapes=[
            pltpu.VMEM((rows, width), bf16),
            pltpu.VMEM((XH * Y * CORE, 2, TILE, TILE), bf16),
            pltpu.VMEM((rows, vectors), bf16),
            pltpu.VMEM((Z * XL, rows, width), bf16),
            pltpu.VMEM((Z * XL, rows, width), bf16),
            pltpu.VMEM((CORE, Y, XH, rows, width), f32),
            pltpu.VMEM((2, Y, XH, rows, width), f32),
            pltpu.VMEM((Y, XH, rows, width), f32),
            pltpu.VMEM((2, Y - 1, XH, rows, width), f32),
            pltpu.VMEM((XH, rows, width), f32),
            pltpu.VMEM((2, rows, width), f32),
            pltpu.VMEM((rows, width), f32),
            pltpu.VMEM((PLANE, chunk, width), f32),
            pltpu.VMEM((PLANE, chunk, width), f32),
            pltpu.VMEM((ZA, chunk, width), f32),
            pltpu.VMEM((ZB, chunk, width), f32),
            pltpu.VMEM((PLANE, chunk, width), f32),
            pltpu.VMEM((PLANE, 1, width), f32),
            pltpu.VMEM((Z, 1, width), f32),
            pltpu.SemaphoreType.DMA((2, 5)),
            pltpu.SemaphoreType.DMA((2, Z * XL)),
            pltpu.SemaphoreType.DMA((2, Y + 1)),
            pltpu.SemaphoreType.DMA((2, Y + 1)),
            pltpu.SemaphoreType.DMA((6,)),
            pltpu.SemaphoreType.DMA((6,)),
            pltpu.SemaphoreType.DMA((4,)),
        ],
        compiler_params=pltpu.CompilerParams(
            collective_id=0, has_side_effects=True, vmem_limit_bytes=56 * 1024 * 1024
        ),
    )(
        tile_columns.reshape(XH * Y * CORE, 2).T,
        start_block,
        matrix_tiles.reshape(XH * Y * CORE, 2, TILE, TILE),
        history,
    )


def solution(mesh):
    split = Mesh(mesh.devices.reshape(XH, Y, CORE, Z, XL), ROW_COL)
    return jax.shard_map(
        per_device,
        mesh=split,
        in_specs=(
            P(ROW_COL, None),
            P(ROW, None, COL, None, None, None),
            P(ROW, None, COL, None),
            P(ROW_COL, None),
        ),
        out_specs=(P(ROW_COL, None), P()),
        check_vma=False,
    )
```

```python
import functools

import jax
import jax.numpy as jnp
from jax import lax
from jax.experimental import pallas as pl
from jax.experimental.pallas import tpu as pltpu
from jax.sharding import Mesh
from jax.sharding import PartitionSpec as P

COL = ("col_0", "col_1")
ROW = ("row_0", "row_1", "row_2")
ROW_COL = ROW + COL
MESH = pl.DeviceIdType.MESH
XH, Y, CORE, Z, XL = 2, 4, 2, 32, 2
ZA = 8
ZB = Z // ZA
PLANE = XH * XL * Y * CORE
TILE = 128
STRIDE = 4


def split3(x):
    hi = x.astype(jnp.bfloat16)
    rest = x - hi.astype(jnp.float32)
    mid = rest.astype(jnp.bfloat16)
    low = (rest - mid.astype(jnp.float32)).astype(jnp.bfloat16)
    return hi, mid, low


def wait_bytes(ref, sem):
    pltpu.make_async_copy(ref, ref, sem).wait()


def kernel(
    states,
    cols,
    start_hbm,
    tiles_hbm,
    hist_hbm,
    out,
    coef_out,
    start,
    tiles,
    hist,
    seg1,
    seg2,
    part,
    core_in,
    upper,
    lower,
    ya_in,
    yb_in,
    xa_in,
    xb_in,
    pair,
    crossed,
    filt,
    proj,
    proj_in,
    za_in,
    zb_in,
    coef,
    sq_plane,
    sq_z,
    ring_send,
    ring_recv,
    row_send,
    row_recv,
    group_send,
    group_recv,
    local_sem,
):
    xh, y, core = (lax.axis_index(a) for a in ROW)
    z, xl = (lax.axis_index(a) for a in COL)

    def along(step):
        return (xh, y, core, lax.rem(z + step + Z, Z), xl)

    across = (xh, y, core, z, 1 - xl)
    place = ((xh * XL + xl) * Y + y) * CORE + core

    def plane_device(q):
        return (
            q // (XL * Y * CORE),
            lax.rem(q // CORE, Y),
            lax.rem(q, CORE),
            z,
            lax.rem(q // (Y * CORE), XL),
        )

    def slot_of(zz):
        return lax.rem(zz + 2 * Z, Z) * XL + xl

    mine = slot_of(z)
    first = pltpu.make_async_copy(start_hbm, seg1.at[mine], local_sem.at[0])
    first.start()
    loads = [
        pltpu.make_async_copy(source, target, local_sem.at[i])
        for i, source, target in (
            (1, tiles_hbm, tiles),
            (2, hist_hbm, hist),
            (3, start_hbm, start),
        )
    ]
    for load in loads:
        load.start()
    barrier = pltpu.get_barrier_semaphore()

    def greet(i, carry):
        device = plane_device(lax.rem(place + i, PLANE))
        pl.semaphore_signal(barrier, inc=1, device_id=device, device_id_type=MESH)
        return carry

    for reach in (STRIDE, 2, 1):
        for device in (along(reach), along(-reach)):
            pl.semaphore_signal(
                barrier, inc=1, device_id=device, device_id_type=MESH
            )
    lax.fori_loop(1, PLANE, greet, 0)
    pl.semaphore_wait(barrier, PLANE + 5)

    def gather(seg, which):
        def send(offset, device, lane):
            slot = slot_of(z + offset)
            pltpu.make_async_remote_copy(
                src_ref=seg.at[slot],
                dst_ref=seg.at[slot],
                send_sem=ring_send.at[which, lane],
                recv_sem=ring_recv.at[which, slot],
                device_id=device,
                device_id_type=MESH,
            ).start()

        def arrived(offset):
            slot = slot_of(z + offset)
            wait_bytes(seg.at[slot], ring_recv.at[which, slot])

        def cross(*offsets):
            for offset in offsets:
                arrived(offset)
                send(offset, across, 4)

        def spread(k):
            for near in (1, -1):
                send(-STRIDE * k, along(near), 2)
                send(STRIDE * k, along(near), 3)
            send(-STRIDE * k, along(2), 2)
            send(STRIDE * k, along(-2), 3)

        def spread_in(k):
            cross(-1 - STRIDE * k, 1 + STRIDE * k, -2 - STRIDE * k, 2 + STRIDE * k)

            @pl.when(k > 0)
            def _():
                cross(-1 + STRIDE * k, 1 - STRIDE * k)

        def step(k, carry):
            arrived(-STRIDE * k)
            send(-STRIDE * k, along(STRIDE), 0)
            arrived(STRIDE * k)
            send(STRIDE * k, along(-STRIDE), 1)
            spread(k)
            send(-STRIDE * k, across, 4)
            send(STRIDE * k, across, 4)
            spread_in(k - 1)
            return carry

        last = Z // 2 // STRIDE - 1
        far = Z // 2
        send(0, along(STRIDE), 0)
        send(0, along(-STRIDE), 1)
        send(0, along(1), 2)
        send(0, along(-1), 3)
        send(0, along(2), 2)
        send(0, along(-2), 3)
        send(0, across, 4)
        lax.fori_loop(1, last, step, 0)
        arrived(-STRIDE * last)
        send(-STRIDE * last, along(STRIDE), 0)
        arrived(STRIDE * last)
        spread(last)
        send(-STRIDE * last, across, 4)
        send(STRIDE * last, across, 4)
        spread_in(jnp.int32(last - 1))
        arrived(-far)
        send(-far, along(1), 2)
        send(-far, along(-1), 3)
        send(-far, across, 4)
        spread_in(jnp.int32(last))
        cross(far - 1, 1 - far)

        def other(zz, carry):
            slot = zz * XL + 1 - xl
            wait_bytes(seg.at[slot], ring_recv.at[which, slot])
            return carry

        lax.fori_loop(0, Z, other, 0)
        wait_bytes(seg.at[pl.ds(0, last + 1)], ring_send.at[which, 0])
        wait_bytes(seg.at[pl.ds(0, last)], ring_send.at[which, 1])
        wait_bytes(seg.at[pl.ds(0, 3 * last + 3)], ring_send.at[which, 2])
        wait_bytes(seg.at[pl.ds(0, 3 * last + 3)], ring_send.at[which, 3])
        wait_bytes(seg.at[pl.ds(0, Z)], ring_send.at[which, 4])

    def multiply(seg, which):
        def blocks(owner_core, yy):
            for xx in range(XH):
                p = (xx * Y + yy) * CORE + owner_core
                left = jnp.concatenate([tiles[p, 0], tiles[p, 1]], axis=1)
                right = jnp.concatenate([seg[cols[0, p]], seg[cols[1, p]]], axis=0)
                yield xx, jnp.dot(left, right, preferred_element_type=jnp.float32)

        def push(source, target, lane, device):
            copy = pltpu.make_async_remote_copy(
                src_ref=source,
                dst_ref=target,
                send_sem=row_send.at[which, lane],
                recv_sem=row_recv.at[which, lane],
                device_id=device,
                device_id_type=MESH,
            )
            copy.start()
            return copy

        def row_of(i):
            return lax.rem(y + i, Y)

        def y_device(i):
            return (xh, row_of(i), core, z, xl)

        other_core = (xh, y, 1 - core, z, xl)
        other_x = (1 - xh, y, core, z, xl)
        order = (2, 1, 3, 0)
        half = TILE // 2
        swaps, y_first, x_first = {}, {}, {}
        for i in order:
            yy = row_of(i)
            for xx, value in blocks(1 - core, yy):
                part[yy, xx] = value
            swaps[i] = push(part.at[yy], core_in.at[which, yy], i, other_core)
        for i in order:
            yy = row_of(i)
            mine_here = list(blocks(core, yy))
            swaps[i].wait_recv()
            for xx, value in mine_here:
                value = value + core_in[which, yy, xx]
                upper[yy, xx] = value[:half]
                lower[yy, xx] = value[half:]
            x_first[i] = push(
                lower.at[yy, 1 - xh], xb_in.at[which, yy], 2 * Y + i, other_x
            )
            if i:
                y_first[i] = push(
                    upper.at[yy], ya_in.at[which, i - 1], Y + i, y_device(i)
                )
        for i in order[:3]:
            y_first[i].wait_recv()
        for xx in range(XH):
            pair[xx] = (
                upper[y, xx]
                + ya_in[which, 0, xx]
                + ya_in[which, 1, xx]
                + ya_in[which, 2, xx]
            )
        x_last = push(pair.at[1 - xh], xa_in.at[which], Y, other_x)
        for i in order:
            x_first[i].wait_recv()
        for yy in range(Y):
            crossed[yy] = lower[yy, xh] + xb_in[which, yy]
        y_last = [
            push(crossed.at[row_of(i)], yb_in.at[which, i - 1], 3 * Y + i, y_device(i))
            for i in order[:3]
        ]
        x_last.wait_recv()
        top = pair[xh] + xa_in[which]
        for copy in y_last:
            copy.wait_recv()
        bottom = crossed[y] + yb_in[which, 0] + yb_in[which, 1] + yb_in[which, 2]
        for copy in (*swaps.values(), *x_first.values(), *y_first.values(), x_last, *y_last):
            copy.wait_send()
        return jnp.concatenate([top, bottom], axis=0)

    first.wait()
    gather(seg1, 0)
    for load in loads:
        load.wait()
    seg2[mine] = multiply(seg1, 0).astype(jnp.bfloat16)
    gather(seg2, 1)
    filtered = 2.0 * multiply(seg2, 1) - start[...].astype(jnp.float32)
    filt[...] = filtered

    def to_group(source, target, group, count, me, device_of, whole):
        def send(i, carry):
            peer = lax.rem(me + i, count)
            pltpu.make_async_remote_copy(
                src_ref=source.at[peer if whole else me],
                dst_ref=target.at[me],
                send_sem=group_send.at[group],
                recv_sem=group_recv.at[group],
                device_id=device_of(peer),
                device_id_type=MESH,
            ).start()
            return carry

        lax.fori_loop(1, count, send, 0)
        wait_bytes(target.at[pl.ds(0, count - 1)], group_recv.at[group])
        wait_bytes(target.at[pl.ds(0, count - 1)], group_send.at[group])

    def sum_of(ref, count):
        total = ref[0]
        for i in range(1, count):
            total = total + ref[i]
        return total

    total = None
    for term in split3(filtered):
        product = lax.dot_general(
            hist[...], term, (((0,), (0,)), ((), ())), preferred_element_type=jnp.float32
        )
        total = product if total is None else total + product
    proj[...] = total.reshape(proj.shape)
    proj_in[place] = proj[place]
    to_group(proj, proj_in, 0, PLANE, place, plane_device, True)

    z_hi, z_lo = z // ZA, lax.rem(z, ZA)
    za_in[z_lo] = sum_of(proj_in, PLANE)
    to_group(za_in, za_in, 1, ZA, z_lo, lambda i: (xh, y, core, z_hi * ZA + i, xl), False)
    zb_in[z_hi] = sum_of(za_in, ZA)
    to_group(zb_in, zb_in, 2, ZB, z_hi, lambda i: (xh, y, core, i * ZA + z_lo, xl), False)
    coef[place] = sum_of(zb_in, ZB)
    to_group(coef, coef, 3, PLANE, place, plane_device, False)
    coeffs = coef[...].reshape(coef_out.shape)
    coef_out[...] = coeffs

    cleaned = filt[...]
    for term in split3(coeffs):
        cleaned = cleaned - jnp.dot(hist[...], term, preferred_element_type=jnp.float32)
    filt[...] = cleaned
    sq_plane[place] = jnp.sum(cleaned * cleaned, axis=0, keepdims=True)
    to_group(sq_plane, sq_plane, 4, PLANE, place, plane_device, False)
    sq_z[z] = sum_of(sq_plane, PLANE)
    to_group(sq_z, sq_z, 5, Z, z, lambda i: (xh, y, core, i, xl), False)
    lengths = jnp.sqrt(sum_of(sq_z, Z) / states + 1e-05)
    out[...] = filt[...] / lengths


def per_device(start_block, matrix_tiles, tile_columns, history):
    rows, width = start_block.shape
    vectors = history.shape[1]
    chunk = vectors // PLANE
    f32, bf16 = jnp.float32, jnp.bfloat16
    vmem = pl.BlockSpec(memory_space=pltpu.VMEM)
    hbm = pl.BlockSpec(memory_space=pl.ANY)
    return pl.pallas_call(
        functools.partial(kernel, float(rows * XH * Y * CORE * Z * XL)),
        out_shape=(
            jax.ShapeDtypeStruct((rows, width), f32),
            jax.ShapeDtypeStruct((vectors, width), f32),
        ),
        in_specs=[pl.BlockSpec(memory_space=pltpu.SMEM), hbm, hbm, hbm],
        out_specs=(vmem, vmem),
        scratch_shapes=[
            pltpu.VMEM((rows, width), bf16),
            pltpu.VMEM((XH * Y * CORE, 2, TILE, TILE), bf16),
            pltpu.VMEM((rows, vectors), bf16),
            pltpu.VMEM((Z * XL, rows, width), bf16),
            pltpu.VMEM((Z * XL, rows, width), bf16),
            pltpu.VMEM((Y, XH, rows, width), f32),
            pltpu.VMEM((2, Y, XH, rows, width), f32),
            pltpu.VMEM((Y, XH, rows // 2, width), f32),
            pltpu.VMEM((Y, XH, rows // 2, width), f32),
            pltpu.VMEM((2, Y - 1, XH, rows // 2, width), f32),
            pltpu.VMEM((2, Y - 1, rows // 2, width), f32),
            pltpu.VMEM((2, rows // 2, width), f32),
            pltpu.VMEM((2, Y, rows // 2, width), f32),
            pltpu.VMEM((XH, rows // 2, width), f32),
            pltpu.VMEM((Y, rows // 2, width), f32),
            pltpu.VMEM((rows, width), f32),
            pltpu.VMEM((PLANE, chunk, width), f32),
            pltpu.VMEM((PLANE, chunk, width), f32),
            pltpu.VMEM((ZA, chunk, width), f32),
            pltpu.VMEM((ZB, chunk, width), f32),
            pltpu.VMEM((PLANE, chunk, width), f32),
            pltpu.VMEM((PLANE, 1, width), f32),
            pltpu.VMEM((Z, 1, width), f32),
            pltpu.SemaphoreType.DMA((2, 5)),
            pltpu.SemaphoreType.DMA((2, Z * XL)),
            pltpu.SemaphoreType.DMA((2, 4 * Y)),
            pltpu.SemaphoreType.DMA((2, 4 * Y)),
            pltpu.SemaphoreType.DMA((6,)),
            pltpu.SemaphoreType.DMA((6,)),
            pltpu.SemaphoreType.DMA((4,)),
        ],
        compiler_params=pltpu.CompilerParams(
            collective_id=0, has_side_effects=True, vmem_limit_bytes=58720256
        ),
    )(
        tile_columns.reshape(XH * Y * CORE, 2).T,
        start_block,
        matrix_tiles.reshape(XH * Y * CORE, 2, TILE, TILE),
        history,
    )


def solution(mesh):
    split = Mesh(mesh.devices.reshape(XH, Y, CORE, Z, XL), ROW_COL)
    return jax.shard_map(
        per_device,
        mesh=split,
        in_specs=(
            P(ROW_COL, None),
            P(ROW, None, COL, None, None, None),
            P(ROW, None, COL, None),
            P(ROW_COL, None),
        ),
        out_specs=(P(ROW_COL, None), P()),
        check_vma=False,
    )
```

```python
import functools

import jax
import jax.numpy as jnp
from jax import lax
from jax.experimental import pallas as pl
from jax.experimental.pallas import tpu as pltpu
from jax.sharding import Mesh
from jax.sharding import PartitionSpec as P

COL = ("col_0", "col_1")
ROW = ("row_0", "row_1", "row_2")
ROW_COL = ROW + COL
MESH = pl.DeviceIdType.MESH
XH, Y, CORE, Z, XL = 2, 4, 2, 32, 2
ZA = 8
ZB = Z // ZA
PLANE = XH * XL * Y * CORE
TILE = 128
STRIDE = 4


def split3(x):
    hi = x.astype(jnp.bfloat16)
    rest = x - hi.astype(jnp.float32)
    mid = rest.astype(jnp.bfloat16)
    low = (rest - mid.astype(jnp.float32)).astype(jnp.bfloat16)
    return hi, mid, low


def wait_bytes(ref, sem):
    pltpu.make_async_copy(ref, ref, sem).wait()


def kernel(
    states,
    cols,
    start_hbm,
    tiles_hbm,
    hist_hbm,
    out,
    coef_out,
    start,
    tiles,
    hist,
    seg1,
    seg2,
    part,
    core_in,
    upper,
    lower,
    ya_in,
    yb_in,
    xa_in,
    xb_in,
    pair,
    crossed,
    filt,
    proj,
    proj_in,
    za_in,
    zb_in,
    coef,
    sq_plane,
    sq_z,
    ring_send,
    ring_recv,
    row_send,
    row_recv,
    group_send,
    group_recv,
    local_sem,
):
    xh, y, core = (lax.axis_index(a) for a in ROW)
    z, xl = (lax.axis_index(a) for a in COL)

    def along(step):
        return (xh, y, core, lax.rem(z + step + Z, Z), xl)

    across = (xh, y, core, z, 1 - xl)
    place = ((xh * XL + xl) * Y + y) * CORE + core

    def plane_device(q):
        return (
            lax.div(q, XL * Y * CORE),
            lax.rem(lax.div(q, CORE), Y),
            lax.rem(q, CORE),
            z,
            lax.rem(lax.div(q, Y * CORE), XL),
        )

    def slot_of(zz):
        return lax.rem(zz + 2 * Z, Z) * XL + xl

    mine = slot_of(z)
    first = pltpu.make_async_copy(start_hbm, seg1.at[mine], local_sem.at[0])
    first.start()
    loads = [
        pltpu.make_async_copy(source, target, local_sem.at[i])
        for i, source, target in (
            (1, tiles_hbm, tiles),
            (2, hist_hbm, hist),
            (3, start_hbm, start),
        )
    ]
    for load in loads:
        load.start()
    barrier = pltpu.get_barrier_semaphore()

    def greet(i, carry):
        device = plane_device(lax.rem(place + i, PLANE))
        pl.semaphore_signal(barrier, inc=1, device_id=device, device_id_type=MESH)
        return carry

    for reach in (STRIDE, 2, 1):
        for device in (along(reach), along(-reach)):
            pl.semaphore_signal(
                barrier, inc=1, device_id=device, device_id_type=MESH
            )
    lax.fori_loop(1, PLANE, greet, 0)
    pl.semaphore_wait(barrier, PLANE + 5)

    unsent = []

    def gather(seg, which):
        def send(offset, device, lane):
            slot = slot_of(z + offset)
            pltpu.make_async_remote_copy(
                src_ref=seg.at[slot],
                dst_ref=seg.at[slot],
                send_sem=ring_send.at[which, lane],
                recv_sem=ring_recv.at[which, slot],
                device_id=device,
                device_id_type=MESH,
            ).start()

        def arrived(offset):
            slot = slot_of(z + offset)
            wait_bytes(seg.at[slot], ring_recv.at[which, slot])

        def cross(*offsets):
            for offset in offsets:
                arrived(offset)
                send(offset, across, 4)

        def spread(k):
            for near in (1, -1):
                send(-STRIDE * k, along(near), 2)
                send(STRIDE * k, along(near), 3)
            send(-STRIDE * k, along(2), 2)
            send(STRIDE * k, along(-2), 3)

        def spread_in(k):
            cross(-1 - STRIDE * k, 1 + STRIDE * k, -2 - STRIDE * k, 2 + STRIDE * k)

            @pl.when(k > 0)
            def _():
                cross(-1 + STRIDE * k, 1 - STRIDE * k)

        def step(k, carry):
            arrived(-STRIDE * k)
            send(-STRIDE * k, along(STRIDE), 0)
            arrived(STRIDE * k)
            send(STRIDE * k, along(-STRIDE), 1)
            spread(k)
            send(-STRIDE * k, across, 4)
            send(STRIDE * k, across, 4)
            spread_in(k - 1)
            return carry

        last = Z // 2 // STRIDE - 1
        far = Z // 2
        send(0, along(STRIDE), 0)
        send(0, along(-STRIDE), 1)
        send(0, along(1), 2)
        send(0, along(-1), 3)
        send(0, along(2), 2)
        send(0, along(-2), 3)
        send(0, across, 4)
        lax.fori_loop(1, last, step, 0)
        arrived(-STRIDE * last)
        send(-STRIDE * last, along(STRIDE), 0)
        arrived(STRIDE * last)
        spread(last)
        send(-STRIDE * last, across, 4)
        send(STRIDE * last, across, 4)
        spread_in(jnp.int32(last - 1))
        arrived(-far)
        send(-far, along(1), 2)
        send(-far, along(-1), 3)
        send(-far, across, 4)
        spread_in(jnp.int32(last))
        cross(far - 1, 1 - far)

        def other(zz, carry):
            slot = zz * XL + 1 - xl
            wait_bytes(seg.at[slot], ring_recv.at[which, slot])
            return carry

        lax.fori_loop(0, Z, other, 0)
        counts = (last + 1, last, 3 * last + 3, 3 * last + 3, Z)
        for lane, count in enumerate(counts):
            unsent.append((seg.at[pl.ds(0, count)], ring_send.at[which, lane]))

    def multiply(seg, which):
        def blocks(owner_core, yy):
            for xx in range(XH):
                p = (xx * Y + yy) * CORE + owner_core
                left = jnp.concatenate([tiles[p, 0], tiles[p, 1]], axis=1)
                right = jnp.concatenate([seg[cols[0, p]], seg[cols[1, p]]], axis=0)
                yield xx, jnp.dot(left, right, preferred_element_type=jnp.float32)

        def push(source, target, lane, device):
            copy = pltpu.make_async_remote_copy(
                src_ref=source,
                dst_ref=target,
                send_sem=row_send.at[which, lane],
                recv_sem=row_recv.at[which, lane],
                device_id=device,
                device_id_type=MESH,
            )
            copy.start()
            return copy

        def row_of(i):
            return lax.rem(y + i, Y)

        def y_device(i):
            return (xh, row_of(i), core, z, xl)

        other_core = (xh, y, 1 - core, z, xl)
        other_x = (1 - xh, y, core, z, xl)
        order = (2, 1, 3, 0)
        half = TILE // 2
        swaps, y_first, x_first = {}, {}, {}
        for i in order:
            yy = row_of(i)
            for xx, value in blocks(1 - core, yy):
                part[yy, xx] = value
            swaps[i] = push(part.at[yy], core_in.at[which, yy], i, other_core)
        for i in order:
            yy = row_of(i)
            mine_here = list(blocks(core, yy))
            swaps[i].wait_recv()
            for xx, value in mine_here:
                value = value + core_in[which, yy, xx]
                upper[yy, xx] = value[:half]
                lower[yy, xx] = value[half:]
            x_first[i] = push(
                lower.at[yy, 1 - xh], xb_in.at[which, yy], 2 * Y + i, other_x
            )
            if i:
                y_first[i] = push(
                    upper.at[yy], ya_in.at[which, i - 1], Y + i, y_device(i)
                )
        for i in order[:3]:
            y_first[i].wait_recv()
        for xx in range(XH):
            pair[xx] = (
                upper[y, xx]
                + ya_in[which, 0, xx]
                + ya_in[which, 1, xx]
                + ya_in[which, 2, xx]
            )
        x_last = push(pair.at[1 - xh], xa_in.at[which], Y, other_x)
        for i in order:
            x_first[i].wait_recv()
        for yy in range(Y):
            crossed[yy] = lower[yy, xh] + xb_in[which, yy]
        y_last = [
            push(crossed.at[row_of(i)], yb_in.at[which, i - 1], 3 * Y + i, y_device(i))
            for i in order[:3]
        ]
        x_last.wait_recv()
        top = pair[xh] + xa_in[which]
        for copy in y_last:
            copy.wait_recv()
        bottom = crossed[y] + yb_in[which, 0] + yb_in[which, 1] + yb_in[which, 2]
        sent = (*swaps.values(), *x_first.values(), *y_first.values(), x_last, *y_last)
        return jnp.concatenate([top, bottom], axis=0), sent

    first.wait()
    gather(seg1, 0)
    for load in loads:
        load.wait()
    first_power, sent = multiply(seg1, 0)
    seg2[mine] = first_power.astype(jnp.bfloat16)
    gather(seg2, 1)
    for copy in sent:
        copy.wait_send()
    second_power, sent = multiply(seg2, 1)
    filtered = 2.0 * second_power - start[...].astype(jnp.float32)
    filt[...] = filtered

    def far_first(i, count):
        return jnp.where(i <= count // 2, count // 2 + 1 - i, i)

    def to_group(source, target, group, count, me, device_of, whole):
        def send(i, carry):
            peer = lax.rem(me + far_first(i, count), count)
            pltpu.make_async_remote_copy(
                src_ref=source.at[peer if whole else me],
                dst_ref=target.at[me],
                send_sem=group_send.at[group],
                recv_sem=group_recv.at[group],
                device_id=device_of(peer),
                device_id_type=MESH,
            ).start()
            return carry

        lax.fori_loop(1, count, send, 0)
        wait_bytes(target.at[pl.ds(0, count - 1)], group_recv.at[group])
        unsent.append((target.at[pl.ds(0, count - 1)], group_send.at[group]))

    def sum_of(ref, count):
        total = ref[0]
        for i in range(1, count):
            total = total + ref[i]
        return total

    total = None
    for term in split3(filtered):
        product = lax.dot_general(
            hist[...], term, (((0,), (0,)), ((), ())), preferred_element_type=jnp.float32
        )
        total = product if total is None else total + product
    proj[...] = total.reshape(proj.shape)
    proj_in[place] = proj[place]
    to_group(proj, proj_in, 0, PLANE, place, plane_device, True)

    z_hi, z_lo = z // ZA, lax.rem(z, ZA)
    za_in[z_lo] = sum_of(proj_in, PLANE)
    to_group(za_in, za_in, 1, ZA, z_lo, lambda i: (xh, y, core, z_hi * ZA + i, xl), False)
    zb_in[z_hi] = sum_of(za_in, ZA)
    to_group(zb_in, zb_in, 2, ZB, z_hi, lambda i: (xh, y, core, i * ZA + z_lo, xl), False)
    coef[place] = sum_of(zb_in, ZB)
    to_group(coef, coef, 3, PLANE, place, plane_device, False)
    coeffs = coef[...].reshape(coef_out.shape)

    cleaned = filt[...]
    for term in split3(coeffs):
        cleaned = cleaned - jnp.dot(hist[...], term, preferred_element_type=jnp.float32)
    filt[...] = cleaned
    sq_plane[place] = jnp.sum(cleaned * cleaned, axis=0, keepdims=True)
    to_group(sq_plane, sq_plane, 4, PLANE, place, plane_device, False)
    coef_out[...] = coef[...].reshape(coef_out.shape)
    sq_z[z] = sum_of(sq_plane, PLANE)
    to_group(sq_z, sq_z, 5, Z, z, lambda i: (xh, y, core, i, xl), False)
    lengths = jnp.sqrt(sum_of(sq_z, Z) / states + 1e-05)
    out[...] = filt[...] / lengths
    for copy in sent:
        copy.wait_send()
    for ref, sem in unsent:
        wait_bytes(ref, sem)


def per_device(start_block, matrix_tiles, tile_columns, history):
    rows, width = start_block.shape
    vectors = history.shape[1]
    chunk = vectors // PLANE
    f32, bf16 = jnp.float32, jnp.bfloat16
    vmem = pl.BlockSpec(memory_space=pltpu.VMEM)
    hbm = pl.BlockSpec(memory_space=pl.ANY)
    return pl.pallas_call(
        functools.partial(kernel, float(rows * XH * Y * CORE * Z * XL)),
        out_shape=(
            jax.ShapeDtypeStruct((rows, width), f32),
            jax.ShapeDtypeStruct((vectors, width), f32),
        ),
        in_specs=[pl.BlockSpec(memory_space=pltpu.SMEM), hbm, hbm, hbm],
        out_specs=(vmem, vmem),
        scratch_shapes=[
            pltpu.VMEM((rows, width), bf16),
            pltpu.VMEM((XH * Y * CORE, 2, TILE, TILE), bf16),
            pltpu.VMEM((rows, vectors), bf16),
            pltpu.VMEM((Z * XL, rows, width), bf16),
            pltpu.VMEM((Z * XL, rows, width), bf16),
            pltpu.VMEM((Y, XH, rows, width), f32),
            pltpu.VMEM((2, Y, XH, rows, width), f32),
            pltpu.VMEM((Y, XH, rows // 2, width), f32),
            pltpu.VMEM((Y, XH, rows // 2, width), f32),
            pltpu.VMEM((2, Y - 1, XH, rows // 2, width), f32),
            pltpu.VMEM((2, Y - 1, rows // 2, width), f32),
            pltpu.VMEM((2, rows // 2, width), f32),
            pltpu.VMEM((2, Y, rows // 2, width), f32),
            pltpu.VMEM((XH, rows // 2, width), f32),
            pltpu.VMEM((Y, rows // 2, width), f32),
            pltpu.VMEM((rows, width), f32),
            pltpu.VMEM((PLANE, chunk, width), f32),
            pltpu.VMEM((PLANE, chunk, width), f32),
            pltpu.VMEM((ZA, chunk, width), f32),
            pltpu.VMEM((ZB, chunk, width), f32),
            pltpu.VMEM((PLANE, chunk, width), f32),
            pltpu.VMEM((PLANE, 1, width), f32),
            pltpu.VMEM((Z, 1, width), f32),
            pltpu.SemaphoreType.DMA((2, 5)),
            pltpu.SemaphoreType.DMA((2, Z * XL)),
            pltpu.SemaphoreType.DMA((2, 4 * Y)),
            pltpu.SemaphoreType.DMA((2, 4 * Y)),
            pltpu.SemaphoreType.DMA((6,)),
            pltpu.SemaphoreType.DMA((6,)),
            pltpu.SemaphoreType.DMA((4,)),
        ],
        compiler_params=pltpu.CompilerParams(
            collective_id=0, has_side_effects=True, vmem_limit_bytes=58720256
        ),
    )(
        tile_columns.reshape(XH * Y * CORE, 2).T,
        start_block,
        matrix_tiles.reshape(XH * Y * CORE, 2, TILE, TILE),
        history,
    )


def solution(mesh):
    split = Mesh(mesh.devices.reshape(XH, Y, CORE, Z, XL), ROW_COL)
    return jax.shard_map(
        per_device,
        mesh=split,
        in_specs=(
            P(ROW_COL, None),
            P(ROW, None, COL, None, None, None),
            P(ROW, None, COL, None),
            P(ROW_COL, None),
        ),
        out_specs=(P(ROW_COL, None), P()),
        check_vma=False,
    )
```
